32 devices in a mesh: tx: 4 (over z), ty: 4 (over y, core), pa: 2 (over x).
Axes of the slice: x: 2, y: 2, z: 4, core: 2. Of those that a mesh axis runs over, the one named last changes fastest.
Arguments:
- object_re: float32 [512, 512], P('tx', 'ty'), may hold values from -4 to 4
- object_im: float32 [512, 512], P('tx', 'ty'), may hold values from -4 to 4
- probe_real: float32 [256, 256], replicated, may hold values from -5 to 5
- probe_imaginary: float32 [256, 256], replicated, may hold values from -5 to 5
- gain: float32 [256, 256], replicated, may hold values from 0.5 to 1.5
- dark: float32 [256, 256], replicated, may hold values from 0.05 to 0.5
- measured: float32 [64, 256, 256], P(('tx', 'ty', 'pa')), may hold values from 0.05 to 5
- positions: int32 [64, 2], P(('tx', 'ty', 'pa')), may hold values from 0 to 511, as said below
- counts: int32 [32], P(('tx', 'ty', 'pa')), may hold values from 1 to 2, as said below
- pixel_good: int32 [256, 256], replicated, may hold values 0 or 1
Outputs:
- new_object_re: float32 [512, 512], P(('tx', 'pa'), 'ty')
- new_object_im: float32 [512, 512], P(('tx', 'pa'), 'ty')
- new_probe_re: float32 [256, 256], replicated
- new_probe_im: float32 [256, 256], replicated
- new_gain: float32 [256, 256], replicated
- new_dark: float32 [256, 256], replicated
The draws below stay inside these ranges and needn't reach their ends.
Inputs may be any that keep to these rules, and one draw needn't show every extreme that they name: `positions`: each pattern's window centre lies in the object tile of the device that holds the slot; the object tile of device (tx, ty, pa) has rows tx * 128 to tx * 128 + 127 and columns ty * 128 to ty * 128 + 127. `counts`: the number of live slots of each device, its first slots.
All inputs are finite; a program needn't handle non-finite values.
Results may differ from the reference program's by a relative error of at most 0.0002.
Values sent between devices are 32-bit elements; how exact they have to be, the bound alone decides.
No kernel may reach another device: no remote copies, remote signals or barrier semaphores. Data moves between devices by JAX's collectives and lax.ppermute only.
A program may use at most 64 MiB of HBM per device.

```python
import math
import jax
import jax.numpy as jnp
from jax import lax

PW = 256
OT = 128
P_CAP = 2
NOR = 512
NOC = 512
PATTERNS = 64
N_TX = 4
N_TY = 4
N_PA = 2
DEVICES = 32


def draw_positions(key, part):
    key_rows, key_cols = jax.random.split(jax.random.fold_in(key, 11))
    slot = jnp.arange(PATTERNS, dtype=jnp.int32)
    device = slot // P_CAP
    tile_row = device // (N_TY * N_PA)
    tile_col = device // N_PA % N_TY
    rows = tile_row * OT + jax.random.randint(key_rows, (PATTERNS,), 0, OT, dtype=jnp.int32)
    cols = tile_col * OT + jax.random.randint(key_cols, (PATTERNS,), 0, OT, dtype=jnp.int32)
    rows = rows.at[0].set(0).at[PATTERNS - 1].set(OT * N_TX - 1)
    cols = cols.at[0].set(0).at[PATTERNS - 1].set(OT * N_TY - 1)
    return jnp.stack([rows, cols], axis=1).astype(jnp.int32)


def draw_counts(key, part):
    key_counts, key_full = jax.random.split(jax.random.fold_in(key, 23))
    values = jax.random.randint(key_counts, (DEVICES,), 1, P_CAP + 1, dtype=jnp.int32)
    busiest = jax.random.randint(key_full, (), 0, DEVICES, dtype=jnp.int32)
    return values.at[busiest].set(P_CAP).astype(jnp.int32)


def set_ends(array, own_key, smallest, largest):
    longest = array.shape.index(max(array.shape))
    spots = []
    for shift in (0, 1):
        where = [jax.random.randint(jax.random.fold_in(own_key, axis), (), 0, length) for axis, length in enumerate(array.shape)]
        where[longest] = (where[longest] + shift) % array.shape[longest]
        spots.append(tuple(where))
    return array.at[spots[0]].set(smallest).at[spots[1]].set(largest)


def steps_of(stream_key, shape, cuts, least, largest):
    loudness = 1.0
    for axis_at, parts in cuts:
        heights = jax.random.uniform(jax.random.fold_in(jax.random.fold_in(stream_key, 6), axis_at), (parts,), jnp.float32, least / len(cuts), largest / len(cuts))
        loudness = loudness * jnp.repeat(jnp.exp(heights), shape[axis_at] // parts).reshape((-1,) + (1,) * (len(shape) - 1 - axis_at))
    return loudness


def noise(stream_key, shape, deviation, limit, shards=(), kind=jnp.bfloat16):
    array = deviation * jax.random.normal(stream_key, shape, jnp.float32)
    if shards:
        array = array * steps_of(stream_key, shape, shards, -0.22, 0.18)
    return jnp.clip(array, -limit, limit).astype(kind)


def setup_inputs(seed: int = 0) -> dict:
    streams_of = jax.random.split(jax.random.key(seed), 11)
    object_re = noise(streams_of[0], (NOR, NOC), 0.7, 4.0, ((0, 4), (1, 4)), jnp.float32)
    object_im = noise(streams_of[1], (NOR, NOC), 0.7, 4.0, ((0, 4), (1, 4)), jnp.float32)
    probe_real = noise(streams_of[2], (PW, PW), 1.0, 5.0, (), jnp.float32)
    probe_imaginary = noise(streams_of[3], (PW, PW), 1.0, 5.0, (), jnp.float32)
    gain = jnp.clip(1.0 + 0.1 * jax.random.normal(streams_of[4], (PW, PW), jnp.float32), 0.5, 1.5)
    dark = jnp.clip(jax.random.uniform(streams_of[5], (PW, PW), jnp.float32, 0.05, 0.5), 0.05, 0.5)
    measured = jnp.clip(jnp.exp(math.log(5.0) - 4.6051702 * jax.random.uniform(streams_of[6], (PATTERNS, PW, PW), jnp.float32) ** steps_of(streams_of[6], (PATTERNS, PW, PW), ((0, 32),), -0.2, 0.2)), 0.05, 5.0)
    positions = draw_positions(jax.random.fold_in(streams_of[10], 71), 0)
    counts = draw_counts(jax.random.fold_in(streams_of[10], 71), 0)
    pixel_good = set_ends((jax.random.randint(streams_of[9], (PW, PW), 0, 16) < 15).astype(jnp.int32), jax.random.fold_in(streams_of[9], 1), 0, 1)
    return dict(object_re=object_re, object_im=object_im, probe_real=probe_real, probe_imaginary=probe_imaginary, gain=gain, dark=dark, measured=measured, positions=positions, counts=counts, pixel_good=pixel_good)


def dft_tables(size):
    index = jnp.arange(size, dtype=jnp.int32)
    product = index[:, None] * index[None, :] % size
    angle = product.astype(jnp.float32) * (2.0 * math.pi / size)
    scale = 1.0 / math.sqrt(size)
    return (jnp.cos(angle) * scale, -jnp.sin(angle) * scale)

def matmul(left, right):
    return jnp.dot(left, right, precision=lax.Precision.HIGHEST, preferred_element_type=jnp.float32)

def complex_product(ar, ai, br, bi):
    return (matmul(ar, br) - matmul(ai, bi), matmul(ar, bi) + matmul(ai, br))

def transform(xr, xi, fourier_table_real, fourier_table_imaginary):
    left_re, left_im = complex_product(fourier_table_real, fourier_table_imaginary, xr, xi)
    return complex_product(left_re, left_im, fourier_table_real, fourier_table_imaginary)

def pattern_contributions(object_window_real, object_window_imaginary, probe_real, probe_imaginary, measured_intensity, gain, dark, valid_pixels, fourier_table_real, fourier_table_imaginary):
    psi_re = probe_real * object_window_real - probe_imaginary * object_window_imaginary
    psi_im = probe_real * object_window_imaginary + probe_imaginary * object_window_real
    far_re, far_im = transform(psi_re, psi_im, fourier_table_real, fourier_table_imaginary)
    inten = far_re * far_re + far_im * far_im
    model_intensity = gain * inten + dark
    residual_values = measured_intensity - model_intensity
    intensity_ratio = valid_pixels * (jnp.sqrt(measured_intensity / model_intensity) - 1.0)
    back_re, back_im = transform(intensity_ratio * far_re, intensity_ratio * far_im, fourier_table_real, -fourier_table_imaginary)
    obj_terms = jnp.stack([probe_real * back_re + probe_imaginary * back_im, probe_real * back_im - probe_imaginary * back_re, probe_real * probe_real + probe_imaginary * probe_imaginary])
    det_terms = jnp.stack([object_window_real * back_re + object_window_imaginary * back_im, object_window_real * back_im - object_window_imaginary * back_re, object_window_real * object_window_real + object_window_imaginary * object_window_imaginary, valid_pixels * residual_values * inten, valid_pixels * inten * inten, valid_pixels * residual_values, valid_pixels])
    return (obj_terms, det_terms)

def reference(object_re, object_im, probe_real, probe_imaginary, gain, dark, measured, positions, counts, pixel_good):
    half = PW // 2
    fourier_table_real, fourier_table_imaginary = dft_tables(PW)
    valid_pixels = pixel_good.astype(jnp.float32)
    padded = jnp.pad(jnp.stack([object_re, object_im]), ((0, 0), (half, half), (half, half)))
    zero = jnp.int32(0)

    def step(slot, carry):
        accum, totals = carry
        device = slot // P_CAP
        live = (slot % P_CAP < counts[device]).astype(jnp.float32)
        row = positions[slot, 0].astype(jnp.int32)
        col = positions[slot, 1].astype(jnp.int32)
        window = lax.dynamic_slice(padded, (zero, row, col), (2, PW, PW))
        obj_terms, det_terms = pattern_contributions(window[0], window[1], probe_real, probe_imaginary, measured[slot], gain, dark, valid_pixels, fourier_table_real, fourier_table_imaginary)
        current = lax.dynamic_slice(accum, (zero, row, col), (3, PW, PW))
        accum = lax.dynamic_update_slice(accum, current + live * obj_terms, (zero, row, col))
        return (accum, totals + live * det_terms)
    accum0 = jnp.zeros((3, NOR + PW, NOC + PW), jnp.float32)
    totals0 = jnp.zeros((7, PW, PW), jnp.float32)
    accum, totals = lax.fori_loop(0, PATTERNS, step, (accum0, totals0))
    inner = accum[:, half:half + NOR, half:half + NOC]
    new_re = object_re + inner[0] / (inner[2] + 0.5)
    new_im = object_im + inner[1] / (inner[2] + 0.5)
    new_probe_re = probe_real + totals[0] / (totals[2] + 0.5)
    new_probe_im = probe_imaginary + totals[1] / (totals[2] + 0.5)
    new_gain = gain + totals[3] / (totals[4] + 1.0)
    new_dark = dark + 0.5 * totals[5] / (totals[6] + 1.0)
    return (new_re, new_im, new_probe_re, new_probe_im, new_gain, new_dark)
```

```python
import functools
import math

import jax
import jax.numpy as jnp
import numpy as np
from jax import lax
from jax.experimental import pallas as pl
from jax.experimental.pallas import tpu as pltpu
from jax.sharding import PartitionSpec as P

MESH_AXES = ("tx", "ty", "pa")
ROWS = 32
SUBLANES = 8


def pairs(size, parity):
    found = []
    for low in range(parity, size - 1, 2):
        found += [(low, low + 1), (low + 1, low)]
    return found


def neighbour_swap(value, axis, parity):
    return lax.ppermute(value, axis, pairs(lax.axis_size(axis), parity))


def ordered(parity, first, second):
    even = parity == 0
    return jnp.where(even, first, second), jnp.where(even, second, first)


def split_table(table):
    high = table.astype(jnp.bfloat16)
    low = (table - high.astype(np.float32)).astype(jnp.bfloat16)
    return high, low


def dft_tables(size):
    index = np.arange(size)
    angle = (np.outer(index, index) % size) * (2.0 * math.pi / size)
    real = (np.cos(angle) / math.sqrt(size)).astype(np.float32)
    imag = (-np.sin(angle) / math.sqrt(size)).astype(np.float32)
    row_form = np.block([[real, imag], [-imag, real]])
    col_form = np.block([[real, -imag], [imag, real]])
    return (*split_table(row_form), *split_table(col_form))


def split(value):
    high = value.astype(jnp.bfloat16)
    return high, (value - high.astype(jnp.float32)).astype(jnp.bfloat16)


def three_pass(left_high, left_low, right_high, right_low):
    dot = functools.partial(jnp.dot, preferred_element_type=jnp.float32)
    return dot(left_high, right_high) + dot(left_high, right_low) + dot(left_low, right_high)


def aligned(row):
    part = lax.rem(row, SUBLANES)
    return row - part, part


def update_kernel(
    offsets,
    live_count,
    padded,
    probe_re,
    probe_im,
    measured,
    gain,
    dark,
    good,
    row_high,
    row_low,
    col_high,
    col_low,
    accum,
    totals,
    win,
    x_high,
    x_low,
    y_high,
    y_low,
    line,
    plane,
):
    slots = measured.shape[0]
    size = probe_re.shape[0]
    side = padded.shape[1]
    steps = size // ROWS
    accum[...] = jnp.zeros_like(accum)
    totals[...] = jnp.zeros_like(totals)

    def right_then_left(first_high, first_low, second_high, second_low):
        for slot in range(slots):
            here = pl.ds(slot * size, size)
            line[...] = three_pass(x_high[here, :], x_low[here, :], first_high[...], first_low[...])
            for part in range(2):
                high, low = split(line[:, part * size : (part + 1) * size])
                y_high[part * size : (part + 1) * size, here] = high
                y_low[part * size : (part + 1) * size, here] = low
        for slot in range(slots):
            here = pl.ds(slot * size, size)
            plane[slot] = three_pass(
                second_high[...], second_low[...], y_high[:, here], y_low[:, here]
            )

    def put_x(slot, at, real, imag):
        rows = pl.ds(slot * size + at, ROWS)
        for part, value in enumerate((real, imag)):
            high, low = split(value)
            x_high[rows, part * size : (part + 1) * size] = high
            x_low[rows, part * size : (part + 1) * size] = low

    for slot in range(slots):
        row, row_part = aligned(offsets[slot, 0])
        back_rows = lax.rem(ROWS + SUBLANES - row_part, ROWS + SUBLANES)
        back_cols = lax.rem(side - offsets[slot, 1], side)

        def load(step, _):
            at = pl.multiple_of(step * ROWS, ROWS)
            here = pl.ds(at, ROWS)
            parts = []
            for part in range(2):
                band = padded[part, pl.ds(pl.multiple_of(row + at, SUBLANES), ROWS + SUBLANES), :]
                band = pltpu.roll(band, back_rows, axis=0)[:ROWS]
                parts.append(pltpu.roll(band, back_cols, axis=1)[:, :size])
                win[slot, part, here, :] = parts[part]
            wr, wi = parts
            pr, pi = probe_re[here, :], probe_im[here, :]
            put_x(slot, at, pr * wr - pi * wi, pr * wi + pi * wr)
            return 0

        lax.fori_loop(0, steps, load, 0)

    right_then_left(row_high, row_low, col_high, col_low)

    for slot in range(slots):
        live = jnp.where(slot < live_count[0], 1.0, 0.0).astype(jnp.float32)

        def detect(step, _):
            at = pl.multiple_of(step * ROWS, ROWS)
            here = pl.ds(at, ROWS)
            fr = plane[slot, here, :]
            fi = plane[slot, pl.ds(size + at, ROWS), :]
            inten = fr * fr + fi * fi
            model = gain[here, :] * inten + dark[here, :]
            seen = measured[slot, here, :]
            valid = good[here, :].astype(jnp.float32)
            ratio = valid * (jnp.sqrt(seen / model) - 1.0)
            put_x(slot, at, ratio * fr, ratio * fi)
            weight = valid * live
            resid = weight * (seen - model)
            wr, wi = win[slot, 0, here, :], win[slot, 1, here, :]
            totals[0, here, :] += live * (wr * wr + wi * wi)
            totals[1, here, :] += resid * inten
            totals[2, here, :] += weight * inten * inten
            totals[3, here, :] += resid
            return 0

        lax.fori_loop(0, steps, detect, 0)

    right_then_left(col_high, col_low, row_high, row_low)

    for slot in range(slots):
        live = jnp.where(slot < live_count[0], 1.0, 0.0).astype(jnp.float32)
        row, row_part = aligned(offsets[slot, 0])
        col = offsets[slot, 1]

        def place(step, _):
            at = pl.multiple_of(step * ROWS, ROWS)
            here = pl.ds(at, ROWS)
            br = live * plane[slot, here, :]
            bi = live * plane[slot, pl.ds(size + at, ROWS), :]
            wr, wi = win[slot, 0, here, :], win[slot, 1, here, :]
            totals[4, here, :] += wr * br + wi * bi
            totals[5, here, :] += wr * bi - wi * br
            pr, pi = probe_re[here, :], probe_im[here, :]
            terms = (pr * br + pi * bi, pr * bi - pi * br, live * (pr * pr + pi * pi))
            there = pl.ds(pl.multiple_of(row + at, SUBLANES), ROWS + SUBLANES)
            for part, term in enumerate(terms):
                wide = jnp.pad(term, ((0, SUBLANES), (0, side - size)))
                wide = pltpu.roll(pltpu.roll(wide, row_part, axis=0), col, axis=1)
                accum[part, there, :] += wide
            return 0

        lax.fori_loop(0, steps, place, 0)


def update(offsets, counts, padded, probe_re, probe_im, measured, gain, dark, good, tables):
    slots, size = measured.shape[:2]
    side = padded.shape[1]
    smem = pl.BlockSpec(memory_space=pltpu.SMEM)
    vmem = pl.BlockSpec(memory_space=pltpu.VMEM)
    return pl.pallas_call(
        update_kernel,
        out_shape=(
            jax.ShapeDtypeStruct((3, side, side), jnp.float32),
            jax.ShapeDtypeStruct((6, size, size), jnp.float32),
        ),
        in_specs=[smem, smem] + [vmem] * 11,
        out_specs=(vmem, vmem),
        scratch_shapes=[
            pltpu.VMEM((slots, 2, size, size), jnp.float32),
            pltpu.VMEM((slots * size, 2 * size), jnp.bfloat16),
            pltpu.VMEM((slots * size, 2 * size), jnp.bfloat16),
            pltpu.VMEM((2 * size, slots * size), jnp.bfloat16),
            pltpu.VMEM((2 * size, slots * size), jnp.bfloat16),
            pltpu.VMEM((size, 2 * size), jnp.float32),
            pltpu.VMEM((slots, 2 * size, size), jnp.float32),
        ],
        compiler_params=pltpu.CompilerParams(vmem_limit_bytes=40 * 1024 * 1024),
    )(offsets, counts, padded, probe_re, probe_im, measured, gain, dark, good, *tables)


def partner_swap(value, partner_of):
    shape = tuple(lax.axis_size(axis) for axis in MESH_AXES)
    moves = []
    for here in np.ndindex(*shape):
        there = partner_of(*here)
        moves.append((int(np.ravel_multi_index(here, shape)), int(np.ravel_multi_index(there, shape))))
    return lax.ppermute(value, MESH_AXES, moves)


def exchange_steps(n_tx, n_ty, n_pa):
    halving = [(lambda t, y, p: (t, y ^ 1, p), lambda t, y, p: y & 1)]
    y_bits = [1 << k for k in range(1, n_ty.bit_length() - 1)]
    p_bits = [1 << k for k in range(n_pa.bit_length() - 1)]

    def along_y(bit):
        return (lambda t, y, p: (t, y ^ bit, p), lambda t, y, p: (y // bit) & 1)

    def along_p(bit):
        return (lambda t, y, p: (t, y, p ^ bit), lambda t, y, p: (p // bit) & 1)

    def by_core(one, two):
        def partner(t, y, p):
            return one[0](t, y, p) if y % 2 == 0 else two[0](t, y, p)

        def bit(t, y, p):
            return jnp.where(y % 2 == 0, one[1](t, y, p), two[1](t, y, p))

        return partner, bit

    shared = min(len(y_bits), len(p_bits))
    ones = [along_p(b) for b in p_bits[:shared]] + [along_y(b) for b in y_bits[:shared]]
    twos = [along_y(b) for b in y_bits[:shared]] + [along_p(b) for b in p_bits[:shared]]
    halving += [by_core(one, two) for one, two in zip(ones, twos)]
    halving += [along_y(b) for b in y_bits[shared:]] + [along_p(b) for b in p_bits[shared:]]
    whole = [
        (lambda t, y, p, b=1 << k: (t ^ b, y, p), None) for k in range(n_tx.bit_length() - 1)
    ]
    return halving, whole


def body(
    object_re,
    object_im,
    probe_real,
    probe_imaginary,
    gain,
    dark,
    measured,
    positions,
    counts,
    pixel_good,
):
    tile_side = object_re.shape[0]
    window = probe_real.shape[0]
    half = window // 2
    tables = dft_tables(window)
    t, y, p = (lax.axis_index(axis) for axis in MESH_AXES)
    n_tx, n_ty, n_pa = (lax.axis_size(axis) for axis in MESH_AXES)

    tile = jnp.stack([object_re, object_im])
    before, after = ordered(
        t % 2, neighbour_swap(tile, "tx", 1), neighbour_swap(tile, "tx", 0)
    )
    strip = jnp.concatenate([before, tile, after], axis=1)
    before, after = ordered(
        y % 2, neighbour_swap(strip, "ty", 1), neighbour_swap(strip, "ty", 0)
    )
    padded = jnp.concatenate([before, strip, after], axis=2)
    anchor = jnp.stack([t * tile_side, y * tile_side]).astype(jnp.int32)
    accum, totals = update(
        positions - anchor,
        counts,
        padded,
        probe_real,
        probe_imaginary,
        measured,
        gain,
        dark,
        pixel_good,
        tables,
    )

    halving, whole = exchange_steps(n_tx, n_ty, n_pa)
    live = jnp.broadcast_to(counts.astype(jnp.float32)[:, None], (8, window))

    def pack(arrays, tail):
        return jnp.concatenate([arrays.reshape(-1, window), tail], axis=0)

    def unpack(flat, kinds):
        return flat[:-8].reshape(kinds, -1, window), flat[-8:]

    sums = totals
    kinds = totals.shape[0]
    bits = []
    for partner, bit in halving:
        upper = bit(t, y, p)
        bits.append(upper)
        rows = sums.shape[1] // 2
        kept = lax.dynamic_slice_in_dim(sums, upper * rows, rows, 1)
        sent = lax.dynamic_slice_in_dim(sums, (1 - upper) * rows, rows, 1)
        got, got_live = unpack(partner_swap(pack(sent, live), partner), kinds)
        sums, live = kept + got, live + got_live
    for partner, _ in whole:
        got, got_live = unpack(partner_swap(pack(sums, live), partner), kinds)
        sums, live = sums + got, live + got_live
    rows = sums.shape[1]
    first = jnp.int32(0)
    span = window
    for upper in bits:
        span //= 2
        first = first + upper * span
    own = lambda array: lax.dynamic_slice_in_dim(array, first, rows, 0)
    valid = own(pixel_good).astype(jnp.float32)
    new = jnp.stack(
        [
            own(probe_real) + sums[4] / (sums[0] + 0.5),
            own(probe_imaginary) + sums[5] / (sums[0] + 0.5),
            own(gain) + sums[1] / (sums[2] + 1.0),
            own(dark) + 0.5 * sums[3] / (valid * live[:1] + 1.0),
        ]
    )
    for (partner, _), upper in zip(halving[::-1], bits[::-1]):
        low, high = ordered(upper, new, partner_swap(new, partner))
        new = jnp.concatenate([low, high], axis=1)

    edge = half + tile_side
    lower, upper = accum[:, :, :half], accum[:, :, edge:]
    even_y, even_t = y % 2 == 0, t % 2 == 0
    inner = accum[:, :, half:edge]
    to_one, to_zero = ordered(y % 2, lower, upper)
    from_one = neighbour_swap(to_one, "ty", 1)
    from_zero = neighbour_swap(to_zero, "ty", 0)
    strip = inner + from_one + from_zero
    lower, upper = strip[:, :half], strip[:, edge:]
    inner = strip[:, half:edge]
    to_one, to_zero = ordered(t % 2, lower, upper)
    from_one = neighbour_swap(to_one, "tx", 1)
    from_zero = neighbour_swap(to_zero, "tx", 0)
    sums = inner + from_one + from_zero
    for k in range(n_pa.bit_length() - 2, -1, -1):
        bit = 1 << k
        rows = sums.shape[1] // 2
        upper = (p // bit) & 1
        kept = lax.dynamic_slice_in_dim(sums, upper * rows, rows, 1)
        sent = lax.dynamic_slice_in_dim(sums, (1 - upper) * rows, rows, 1)
        sums = kept + lax.ppermute(sent, "pa", [(i, i ^ bit) for i in range(n_pa)])
    rows = sums.shape[1]
    own_tile = lax.dynamic_slice_in_dim(tile, p * rows, rows, 1)
    new_re = own_tile[0] + sums[0] / (sums[2] + 0.5)
    new_im = own_tile[1] + sums[1] / (sums[2] + 0.5)
    return (new_re, new_im, new[0], new[1], new[2], new[3])


def solution(mesh):
    placed = (
        P("tx", "ty"),
        P("tx", "ty"),
        P(),
        P(),
        P(),
        P(),
        P(("tx", "ty", "pa"), None, None),
        P(("tx", "ty", "pa"), None),
        P(("tx", "ty", "pa")),
        P(),
    )
    return jax.shard_map(
        body,
        mesh=mesh,
        in_specs=placed,
        out_specs=(P(("tx", "pa"), "ty"), P(("tx", "pa"), "ty"), P(), P(), P(), P()),
        check_vma=False,
    )
```

```python
import functools
import math

import jax
import jax.numpy as jnp
import numpy as np
from jax import lax
from jax.experimental import pallas as pl
from jax.experimental.pallas import tpu as pltpu
from jax.sharding import PartitionSpec as P


MESH_AXES = ("tx", "ty", "pa")
ROWS = 32
SUBLANES = 8


def partner_swap(value, partner_of):
    shape = tuple(lax.axis_size(axis) for axis in MESH_AXES)
    moves = []
    for here in np.ndindex(*shape):
        there = partner_of(*here)
        if there != here:
            source, target = (int(np.ravel_multi_index(at, shape)) for at in (here, there))
            moves.append((source, target))
    return lax.ppermute(value, MESH_AXES, moves)


def neighbour_swap(value, axis, parity):
    dim = MESH_AXES.index(axis)
    size = lax.axis_size(axis)
    n_pa = lax.axis_size("pa")

    def paired(at):
        other = (at - parity ^ 1) + parity
        return other if 0 <= other < size else None

    def partner(*here):
        other = paired(here[dim])
        if other is None:
            idle = here[2] ^ 1
            return (here[0], here[1], idle if idle < n_pa else here[2])
        return tuple(other if k == dim else at for k, at in enumerate(here))

    got = partner_swap(value, partner)
    if all(paired(at) is not None for at in range(size)):
        return got
    other = (lax.axis_index(axis) - parity ^ 1) + parity
    return jnp.where((0 <= other) & (other < size), got, 0.0)


def ordered(parity, first, second):
    even = parity == 0
    return jnp.where(even, first, second), jnp.where(even, second, first)


def split_table(table):
    high = table.astype(jnp.bfloat16)
    low = (table - high.astype(np.float32)).astype(jnp.bfloat16)
    return high, low


def dft_tables(size):
    index = np.arange(size)
    angle = (np.outer(index, index) % size) * (2.0 * math.pi / size)
    real = (np.cos(angle) / math.sqrt(size)).astype(np.float32)
    imag = (-np.sin(angle) / math.sqrt(size)).astype(np.float32)
    row_form = np.block([[real, imag], [-imag, real]])
    col_form = np.block([[real, -imag], [imag, real]])
    return (*split_table(row_form), *split_table(col_form))


def split(value):
    high = value.astype(jnp.bfloat16)
    return high, (value - high.astype(jnp.float32)).astype(jnp.bfloat16)


def three_pass(left_high, left_low, right_high, right_low):
    dot = functools.partial(jnp.dot, preferred_element_type=jnp.float32)
    return dot(left_high, right_high) + dot(left_high, right_low) + dot(left_low, right_high)


def aligned(row):
    part = lax.rem(row, SUBLANES)
    return row - part, part


def right_then_left(first_high, first_low, second_high, second_low, x_high, x_low, y_high, y_low, line, plane):
    slots, _, size = plane.shape
    for slot in range(slots):
        here = pl.ds(slot * size, size)
        line[...] = three_pass(x_high[here, :], x_low[here, :], first_high[...], first_low[...])
        for part in range(2):
            high, low = split(line[:, part * size : (part + 1) * size])
            y_high[part * size : (part + 1) * size, here] = high
            y_low[part * size : (part + 1) * size, here] = low
        plane[slot] = three_pass(second_high[...], second_low[...], y_high[:, here], y_low[:, here])


def put_x(x_high, x_low, slot, size, at, real, imag):
    rows = pl.ds(slot * size + at, ROWS)
    for part, value in enumerate((real, imag)):
        high, low = split(value)
        x_high[rows, part * size : (part + 1) * size] = high
        x_low[rows, part * size : (part + 1) * size] = low


def put_sums(sums, info, step, values):
    blocks, _, size = sums.shape
    span = size // blocks
    half = blocks // 2
    for sub in range(ROWS // span):
        block = step * (ROWS // span) + sub
        mine = lax.bitwise_xor(block, info[1])
        place = jnp.where(mine < half, mine, half + lax.bitwise_xor(block, info[2]))
        for kind, value in enumerate(values):
            sums[place, kind * span : (kind + 1) * span, :] = value[sub * span : (sub + 1) * span]


def forward_kernel(
    offsets,
    info,
    padded,
    probe_re,
    probe_im,
    row_high,
    row_low,
    col_high,
    col_low,
    measured_hbm,
    gain_hbm,
    dark_hbm,
    good_hbm,
    kept,
    sent,
    x_high,
    x_low,
    win,
    sums,
    measured,
    gain,
    dark,
    good,
    sem,
    y_high,
    y_low,
    line,
    plane,
):
    slots = measured.shape[0]
    size = probe_re.shape[0]
    side = padded.shape[1]
    steps = size // ROWS
    copies = [
        pltpu.make_async_copy(source, target, sem.at[k])
        for k, (source, target) in enumerate(
            ((measured_hbm, measured), (gain_hbm, gain), (dark_hbm, dark), (good_hbm, good))
        )
    ]
    for copy in copies:
        copy.start()

    for slot in range(slots):
        row, row_part = aligned(offsets[slot, 0])
        back_rows = lax.rem(ROWS + SUBLANES - row_part, ROWS + SUBLANES)
        back_cols = lax.rem(side - offsets[slot, 1], side)

        def load(step, _):
            at = pl.multiple_of(step * ROWS, ROWS)
            here = pl.ds(at, ROWS)
            parts = []
            for part in range(2):
                band = padded[part, pl.ds(pl.multiple_of(row + at, SUBLANES), ROWS + SUBLANES), :]
                band = pltpu.roll(band, back_rows, axis=0)[:ROWS]
                parts.append(pltpu.roll(band, back_cols, axis=1)[:, :size])
                win[slot, part, here, :] = parts[part]
            wr, wi = parts
            pr, pi = probe_re[here, :], probe_im[here, :]
            put_x(x_high, x_low, slot, size, at, pr * wr - pi * wi, pr * wi + pi * wr)
            return 0

        lax.fori_loop(0, steps, load, 0)

    right_then_left(
        row_high, row_low, col_high, col_low, x_high, x_low, y_high, y_low, line, plane
    )
    for copy in copies:
        copy.wait()
    blocks, depth, _ = sums.shape
    live_rows = jnp.full((SUBLANES, size), info[0].astype(jnp.float32), jnp.float32)
    for block in range(blocks):
        sums[block, depth - SUBLANES :, :] = live_rows

    def detect(step, _):
        at = pl.multiple_of(step * ROWS, ROWS)
        here = pl.ds(at, ROWS)
        valid = good[here, :].astype(jnp.float32)
        values = [0.0] * 4
        for slot in range(slots):
            live = jnp.where(slot < info[0], 1.0, 0.0).astype(jnp.float32)
            fr = plane[slot, here, :]
            fi = plane[slot, pl.ds(size + at, ROWS), :]
            inten = fr * fr + fi * fi
            model = gain[here, :] * inten + dark[here, :]
            seen = measured[slot, here, :]
            ratio = valid * (jnp.sqrt(seen / model) - 1.0)
            put_x(x_high, x_low, slot, size, at, ratio * fr, ratio * fi)
            weight = valid * live
            resid = weight * (seen - model)
            wr, wi = win[slot, 0, here, :], win[slot, 1, here, :]
            terms = (live * (wr * wr + wi * wi), resid * inten, weight * inten * inten, resid)
            values = [value + term for value, term in zip(values, terms)]
        put_sums(sums, info, step, values)
        return 0

    lax.fori_loop(0, steps, detect, 0)
    kept[...] = sums[: blocks // 2]
    sent[...] = sums[blocks // 2 :]


def backward_kernel(
    offsets,
    info,
    x_high,
    x_low,
    win,
    probe_re,
    probe_im,
    row_high,
    row_low,
    col_high,
    col_low,
    kept,
    sent,
    to_one,
    inner,
    to_zero,
    sums,
    accum,
    y_high,
    y_low,
    line,
    plane,
):
    slots, _, size, _ = win.shape
    side = accum.shape[1]
    tile = inner.shape[2]
    half = to_one.shape[2]
    steps = size // ROWS
    accum[...] = jnp.zeros_like(accum)
    right_then_left(
        col_high, col_low, row_high, row_low, x_high, x_low, y_high, y_low, line, plane
    )

    def place(step, _):
        at = pl.multiple_of(step * ROWS, ROWS)
        here = pl.ds(at, ROWS)
        pr, pi = probe_re[here, :], probe_im[here, :]
        power = pr * pr + pi * pi
        values = [0.0] * 2
        for slot in range(slots):
            live = jnp.where(slot < info[0], 1.0, 0.0).astype(jnp.float32)
            row, row_part = aligned(offsets[slot, 0])
            col = offsets[slot, 1]
            br = live * plane[slot, here, :]
            bi = live * plane[slot, pl.ds(size + at, ROWS), :]
            wr, wi = win[slot, 0, here, :], win[slot, 1, here, :]
            values = [values[0] + wr * br + wi * bi, values[1] + wr * bi - wi * br]
            there = pl.ds(pl.multiple_of(row + at, SUBLANES), ROWS + SUBLANES)
            for part, term in enumerate((pr * br + pi * bi, pr * bi - pi * br, live * power)):
                wide = jnp.pad(term, ((0, SUBLANES), (0, side - size)))
                wide = pltpu.roll(pltpu.roll(wide, row_part, axis=0), col, axis=1)
                accum[part, there, :] += wide
        put_sums(sums, info, step, values)
        return 0

    lax.fori_loop(0, steps, place, 0)
    kept[...] = sums[: sums.shape[0] // 2]
    sent[...] = sums[sums.shape[0] // 2 :]
    odd = info[3] == 1
    inner[...] = accum[:, :, half : half + tile]

    @pl.when(odd)
    def _():
        to_one[...] = accum[:, :, half + tile :]
        to_zero[...] = accum[:, :, :half]

    @pl.when(jnp.logical_not(odd))
    def _():
        to_one[...] = accum[:, :, :half]
        to_zero[...] = accum[:, :, half + tile :]


SMEM = pl.BlockSpec(memory_space=pltpu.SMEM)
VMEM = pl.BlockSpec(memory_space=pltpu.VMEM)
ANY = pl.BlockSpec(memory_space=pl.ANY)


def work_buffers(slots, size):
    return [
        pltpu.VMEM((2 * size, slots * size), jnp.bfloat16),
        pltpu.VMEM((2 * size, slots * size), jnp.bfloat16),
        pltpu.VMEM((size, 2 * size), jnp.float32),
        pltpu.VMEM((slots, 2 * size, size), jnp.float32),
    ]


def kernel_options(slots, size):
    return dict(
        compiler_params=pltpu.CompilerParams(vmem_limit_bytes=24 * 1024 * 1024),
        cost_estimate=pl.CostEstimate(
            flops=slots * 48 * size**3, bytes_accessed=6 * 1024 * 1024, transcendentals=0
        ),
    )


def forward(offsets, info, padded, probe_re, probe_im, tables, measured, gain, dark, good, blocks):
    slots, size = measured.shape[:2]
    depth = 4 * (size // blocks) + SUBLANES
    return pl.pallas_call(
        forward_kernel,
        out_shape=(
            jax.ShapeDtypeStruct((blocks // 2, depth, size), jnp.float32),
            jax.ShapeDtypeStruct((blocks // 2, depth, size), jnp.float32),
            jax.ShapeDtypeStruct((slots * size, 2 * size), jnp.bfloat16),
            jax.ShapeDtypeStruct((slots * size, 2 * size), jnp.bfloat16),
            jax.ShapeDtypeStruct((slots, 2, size, size), jnp.float32),
        ),
        in_specs=[SMEM] * 2 + [VMEM] * 7 + [ANY] * 4,
        out_specs=(VMEM,) * 5,
        scratch_shapes=[
            pltpu.VMEM((blocks, depth, size), jnp.float32),
            pltpu.VMEM((slots, size, size), jnp.float32),
            pltpu.VMEM((size, size), jnp.float32),
            pltpu.VMEM((size, size), jnp.float32),
            pltpu.VMEM((size, size), jnp.int32),
            pltpu.SemaphoreType.DMA((4,)),
            *work_buffers(slots, size),
        ],
        name="forward",
        **kernel_options(slots, size),
    )(offsets, info, padded, probe_re, probe_im, *tables, measured, gain, dark, good)


def backward(offsets, info, x_high, x_low, win, probe_re, probe_im, tables, tile, blocks):
    slots, _, size, _ = win.shape
    half = size // 2
    side = tile + size
    depth = 2 * (size // blocks)
    return pl.pallas_call(
        backward_kernel,
        out_shape=(
            jax.ShapeDtypeStruct((blocks // 2, depth, size), jnp.float32),
            jax.ShapeDtypeStruct((blocks // 2, depth, size), jnp.float32),
            jax.ShapeDtypeStruct((3, side, half), jnp.float32),
            jax.ShapeDtypeStruct((3, side, tile), jnp.float32),
            jax.ShapeDtypeStruct((3, side, half), jnp.float32),
        ),
        in_specs=[SMEM] * 2 + [VMEM] * 9,
        out_specs=(VMEM,) * 5,
        scratch_shapes=[
            pltpu.VMEM((blocks, depth, size), jnp.float32),
            pltpu.VMEM((3, side, side), jnp.float32),
            *work_buffers(slots, size),
        ],
        name="backward",
        **kernel_options(slots, size),
    )(offsets, info, x_high, x_low, win, probe_re, probe_im, *tables)


def exchange_steps(n_tx, n_ty, n_pa):
    def along(dim, bit):
        def partner(*here):
            return tuple(at ^ bit if k == dim else at for k, at in enumerate(here))

        def upper(*here):
            return (here[dim] // bit) & 1

        return partner, upper

    def by_core(one, two):
        def partner(t, y, p):
            return one[0](t, y, p) if y % 2 == 0 else two[0](t, y, p)

        def upper(t, y, p):
            return jnp.where(y % 2 == 0, one[1](t, y, p), two[1](t, y, p))

        return partner, upper

    tx, ty, pa = (
        [along(dim, 1 << k) for k in range(low, size.bit_length() - 1)]
        for dim, (low, size) in enumerate(((0, n_tx), (1, n_ty), (0, n_pa)))
    )
    halving = [along(1, 1)]
    whole = []
    while tx and pa and len(halving) < 3:
        one, two = pa.pop(0), tx.pop(0)
        halving += [by_core(one, two), by_core(two, one)]
    while tx and ty:
        one, two = ty.pop(0), tx.pop(0)
        whole += [by_core(one, two), by_core(two, one)]
    whole += tx + ty + pa
    return halving, whole


def update(
    object_re,
    object_im,
    probe_real,
    probe_imaginary,
    gain,
    dark,
    measured,
    positions,
    counts,
    pixel_good,
):
    tile_side = object_re.shape[0]
    window = probe_real.shape[0]
    half = window // 2
    tables = dft_tables(window)
    t, y, p = (lax.axis_index(axis) for axis in MESH_AXES)
    n_tx, n_ty, n_pa = (lax.axis_size(axis) for axis in MESH_AXES)

    tile = lax.optimization_barrier(jnp.stack([object_re, object_im]))
    near = neighbour_swap(tile, "tx", 0)
    far = neighbour_swap(tile, "tx", 1)
    before, after = ordered(t % 2, far, near)
    strip = jnp.concatenate([before, tile, after], axis=1)
    near = neighbour_swap(strip, "ty", 0)
    far = neighbour_swap(strip, "ty", 1)
    before, after = ordered(y % 2, far, near)
    padded = jnp.concatenate([before, strip, after], axis=2)
    anchor = jnp.stack([t * tile_side, y * tile_side]).astype(jnp.int32)
    offsets = positions - anchor

    halving, whole = exchange_steps(n_tx, n_ty, n_pa)
    blocks = 1 << len(halving)
    span = window // blocks

    def block_of(t, y, p):
        place = jnp.int32(0)
        for _, bit in halving:
            place = 2 * place + bit(t, y, p)
        return place

    mine = block_of(t, y, p)
    other = block_of(*halving[0][0](t, y, p))
    info = jnp.stack([counts[0], mine, other, y % 2]).astype(jnp.int32)
    *early, x_high, x_low, win = forward(
        offsets, info, padded, probe_real, probe_imaginary, tables,
        measured, gain, dark, pixel_good, blocks,
    )
    *late, to_one, inner, to_zero = backward(
        offsets, info, x_high, x_low, win, probe_real, probe_imaginary, tables,
        tile_side, blocks,
    )

    def total(kept, sent):
        for k, (partner, _) in enumerate(halving):
            if k:
                middle = sums.shape[0] // 2
                kept, sent = sums[:middle], sums[middle:]
            sums = kept + partner_swap(sent, partner)
        for partner, _ in whole:
            sums = sums + partner_swap(sums, partner)
        return sums[0]

    def own(array):
        return lax.dynamic_slice_in_dim(array, mine * span, span, 0)

    early = total(*early)
    late = total(*late).reshape(2, span, window)
    power, gain_num, gain_den, dark_num = early[: 4 * span].reshape(4, span, window)
    dark_den = own(pixel_good).astype(jnp.float32) * early[4 * span : 4 * span + 1]
    new = jnp.stack(
        [
            own(probe_real) + late[0] / (power + 0.5),
            own(probe_imaginary) + late[1] / (power + 0.5),
            own(gain) + gain_num / (gain_den + 1.0),
            own(dark) + 0.5 * dark_num / (dark_den + 1.0),
        ]
    )
    for k, (partner, bit) in reversed(list(enumerate(halving))):
        low, high = ordered(bit(t, y, p), new, partner_swap(new, partner))
        new = jnp.concatenate([low, high], axis=1)

    edge = half + tile_side
    strip = inner + neighbour_swap(to_zero, "ty", 0) + neighbour_swap(to_one, "ty", 1)
    to_one, to_zero = ordered(t % 2, strip[:, :half], strip[:, edge:])
    sums = (
        strip[:, half:edge]
        + neighbour_swap(to_zero, "tx", 0)
        + neighbour_swap(to_one, "tx", 1)
    )
    for k in range(n_pa.bit_length() - 2, -1, -1):
        bit = 1 << k
        rows = sums.shape[1] // 2
        upper = (p // bit) & 1
        kept = lax.dynamic_slice_in_dim(sums, upper * rows, rows, 1)
        sent = lax.dynamic_slice_in_dim(sums, (1 - upper) * rows, rows, 1)
        sums = kept + lax.ppermute(sent, "pa", [(i, i ^ bit) for i in range(n_pa)])
    rows = sums.shape[1]
    own_tile = lax.dynamic_slice_in_dim(tile, p * rows, rows, 1)
    new_re = own_tile[0] + sums[0] / (sums[2] + 0.5)
    new_im = own_tile[1] + sums[1] / (sums[2] + 0.5)
    return (new_re, new_im, new[0], new[1], new[2], new[3])


def solution(mesh):
    placed = (
        P("tx", "ty"),
        P("tx", "ty"),
        P(),
        P(),
        P(),
        P(),
        P(("tx", "ty", "pa"), None, None),
        P(("tx", "ty", "pa"), None),
        P(("tx", "ty", "pa")),
        P(),
    )
    return jax.shard_map(
        update,
        mesh=mesh,
        in_specs=placed,
        out_specs=(P(("tx", "pa"), "ty"), P(("tx", "pa"), "ty"), P(), P(), P(), P()),
        check_vma=False,
    )
```

```python
import functools
import math

import jax
import jax.numpy as jnp
import numpy as np
from jax import lax
from jax.experimental import pallas as pl
from jax.experimental.pallas import tpu as pltpu
from jax.sharding import PartitionSpec as P


MESH_AXES = ("tx", "ty", "pa")
ROWS = 32
SUBLANES = 8


def partner_swap(value, partner_of):
    shape = tuple(lax.axis_size(axis) for axis in MESH_AXES)
    moves = []
    for here in np.ndindex(*shape):
        there = partner_of(*here)
        if there != here:
            source, target = (int(np.ravel_multi_index(at, shape)) for at in (here, there))
            moves.append((source, target))
    return lax.ppermute(value, MESH_AXES, moves)


def neighbour_swap(value, axis, parity, fill=True):
    dim = MESH_AXES.index(axis)
    size = lax.axis_size(axis)
    n_pa = lax.axis_size("pa")

    def paired(at):
        other = (at - parity ^ 1) + parity
        return other if 0 <= other < size else None

    def partner(*here):
        other = paired(here[dim])
        if other is None:
            idle = here[2] ^ 1
            return (here[0], here[1], idle if fill and idle < n_pa else here[2])
        return tuple(other if k == dim else at for k, at in enumerate(here))

    got = partner_swap(value, partner)
    if not fill or all(paired(at) is not None for at in range(size)):
        return got
    other = (lax.axis_index(axis) - parity ^ 1) + parity
    return jnp.where((0 <= other) & (other < size), got, 0.0)


def ordered(parity, first, second):
    even = parity == 0
    return jnp.where(even, first, second), jnp.where(even, second, first)


def split_table(table):
    high = table.astype(jnp.bfloat16)
    low = (table - high.astype(np.float32)).astype(jnp.bfloat16)
    return high, low


def dft_tables(size):
    index = np.arange(size)
    angle = (np.outer(index, index) % size) * (2.0 * math.pi / size)
    real = (np.cos(angle) / math.sqrt(size)).astype(np.float32)
    imag = (-np.sin(angle) / math.sqrt(size)).astype(np.float32)
    row_form = np.block([[real, imag], [-imag, real]])
    col_form = np.block([[real, -imag], [imag, real]])
    return (*split_table(row_form), *split_table(col_form))


def split(value):
    high = value.astype(jnp.bfloat16)
    return high, (value - high.astype(jnp.float32)).astype(jnp.bfloat16)


def three_pass(left_high, left_low, right_high, right_low):
    dot = functools.partial(jnp.dot, preferred_element_type=jnp.float32)
    return dot(left_high, right_high) + dot(left_high, right_low) + dot(left_low, right_high)


def aligned(row):
    part = lax.rem(row, SUBLANES)
    return row - part, part


def right_then_left(first_high, first_low, second_high, second_low, x_high, x_low, y_high, y_low, line, plane):
    slots, _, size = plane.shape
    for slot in range(slots):
        here = pl.ds(slot * size, size)
        line[...] = three_pass(x_high[here, :], x_low[here, :], first_high[...], first_low[...])
        for part in range(2):
            high, low = split(line[:, part * size : (part + 1) * size])
            y_high[part * size : (part + 1) * size, here] = high
            y_low[part * size : (part + 1) * size, here] = low
        plane[slot] = three_pass(second_high[...], second_low[...], y_high[:, here], y_low[:, here])


def put_x(x_high, x_low, slot, size, at, real, imag):
    rows = pl.ds(slot * size + at, ROWS)
    for part, value in enumerate((real, imag)):
        high, low = split(value)
        x_high[rows, part * size : (part + 1) * size] = high
        x_low[rows, part * size : (part + 1) * size] = low


def put_sums(sums, info, step, values):
    blocks, _, size = sums.shape
    span = size // blocks
    half = blocks // 2
    for sub in range(ROWS // span):
        block = step * (ROWS // span) + sub
        mine = lax.bitwise_xor(block, info[1])
        place = jnp.where(mine < half, mine, half + lax.bitwise_xor(block, info[2]))
        for kind, value in enumerate(values):
            sums[place, kind * span : (kind + 1) * span, :] = value[sub * span : (sub + 1) * span]


def forward_kernel(
    offsets,
    info,
    padded,
    probe_re,
    probe_im,
    row_high,
    row_low,
    col_high,
    col_low,
    measured_hbm,
    gain_hbm,
    dark_hbm,
    good_hbm,
    kept,
    sent,
    x_high,
    x_low,
    win,
    sums,
    measured,
    gain,
    dark,
    good,
    sem,
    y_high,
    y_low,
    line,
    plane,
):
    slots = measured.shape[0]
    size = probe_re.shape[0]
    side = padded.shape[1]
    steps = size // ROWS
    copies = [
        pltpu.make_async_copy(source, target, sem.at[k])
        for k, (source, target) in enumerate(
            ((measured_hbm, measured), (gain_hbm, gain), (dark_hbm, dark), (good_hbm, good))
        )
    ]
    for copy in copies:
        copy.start()

    for slot in range(slots):
        row, row_part = aligned(offsets[slot, 0])
        back_rows = lax.rem(ROWS + SUBLANES - row_part, ROWS + SUBLANES)
        back_cols = lax.rem(side - offsets[slot, 1], side)

        def load(step, _):
            at = pl.multiple_of(step * ROWS, ROWS)
            here = pl.ds(at, ROWS)
            parts = []
            for part in range(2):
                band = padded[part, pl.ds(pl.multiple_of(row + at, SUBLANES), ROWS + SUBLANES), :]
                band = pltpu.roll(band, back_rows, axis=0)[:ROWS]
                parts.append(pltpu.roll(band, back_cols, axis=1)[:, :size])
                win[slot, part, here, :] = parts[part]
            wr, wi = parts
            pr, pi = probe_re[here, :], probe_im[here, :]
            put_x(x_high, x_low, slot, size, at, pr * wr - pi * wi, pr * wi + pi * wr)
            return 0

        lax.fori_loop(0, steps, load, 0)

    right_then_left(
        row_high, row_low, col_high, col_low, x_high, x_low, y_high, y_low, line, plane
    )
    for copy in copies:
        copy.wait()
    blocks, depth, _ = sums.shape
    live_rows = jnp.full((SUBLANES, size), info[0].astype(jnp.float32), jnp.float32)
    for block in range(blocks):
        sums[block, depth - SUBLANES :, :] = live_rows

    def detect(step, _):
        at = pl.multiple_of(step * ROWS, ROWS)
        here = pl.ds(at, ROWS)
        valid = good[here, :].astype(jnp.float32)
        values = [0.0] * 4
        for slot in range(slots):
            live = jnp.where(slot < info[0], 1.0, 0.0).astype(jnp.float32)
            fr = plane[slot, here, :]
            fi = plane[slot, pl.ds(size + at, ROWS), :]
            inten = fr * fr + fi * fi
            model = gain[here, :] * inten + dark[here, :]
            seen = measured[slot, here, :]
            ratio = valid * (jnp.sqrt(seen / model) - 1.0)
            put_x(x_high, x_low, slot, size, at, ratio * fr, ratio * fi)
            weight = valid * live
            resid = weight * (seen - model)
            wr, wi = win[slot, 0, here, :], win[slot, 1, here, :]
            terms = (live * (wr * wr + wi * wi), resid * inten, weight * inten * inten, resid)
            values = [value + term for value, term in zip(values, terms)]
        put_sums(sums, info, step, values)
        return 0

    lax.fori_loop(0, steps, detect, 0)
    kept[...] = sums[: blocks // 2]
    sent[...] = sums[blocks // 2 :]


def backward_kernel(
    offsets,
    info,
    x_high,
    x_low,
    win,
    probe_re,
    probe_im,
    row_high,
    row_low,
    col_high,
    col_low,
    kept,
    sent,
    to_one,
    inner,
    to_zero,
    sums,
    accum,
    y_high,
    y_low,
    line,
    plane,
):
    slots, _, size, _ = win.shape
    side = accum.shape[1]
    tile = inner.shape[2]
    half = to_one.shape[2]
    steps = size // ROWS
    accum[...] = jnp.zeros_like(accum)
    right_then_left(
        col_high, col_low, row_high, row_low, x_high, x_low, y_high, y_low, line, plane
    )

    def place(step, _):
        at = pl.multiple_of(step * ROWS, ROWS)
        here = pl.ds(at, ROWS)
        pr, pi = probe_re[here, :], probe_im[here, :]
        power = pr * pr + pi * pi
        values = [0.0] * 2
        for slot in range(slots):
            live = jnp.where(slot < info[0], 1.0, 0.0).astype(jnp.float32)
            row, row_part = aligned(offsets[slot, 0])
            col = offsets[slot, 1]
            br = live * plane[slot, here, :]
            bi = live * plane[slot, pl.ds(size + at, ROWS), :]
            wr, wi = win[slot, 0, here, :], win[slot, 1, here, :]
            values = [values[0] + wr * br + wi * bi, values[1] + wr * bi - wi * br]
            there = pl.ds(pl.multiple_of(row + at, SUBLANES), ROWS + SUBLANES)
            for part, term in enumerate((pr * br + pi * bi, pr * bi - pi * br, live * power)):
                wide = jnp.pad(term, ((0, SUBLANES), (0, side - size)))
                wide = pltpu.roll(pltpu.roll(wide, row_part, axis=0), col, axis=1)
                accum[part, there, :] += wide
        put_sums(sums, info, step, values)
        return 0

    lax.fori_loop(0, steps, place, 0)
    kept[...] = sums[: sums.shape[0] // 2]
    sent[...] = sums[sums.shape[0] // 2 :]
    odd = info[3] == 1
    inner[...] = accum[:, :, half : half + tile]

    @pl.when(odd)
    def _():
        to_one[...] = accum[:, :, half + tile :]
        to_zero[...] = accum[:, :, :half]

    @pl.when(jnp.logical_not(odd))
    def _():
        to_one[...] = accum[:, :, :half]
        to_zero[...] = accum[:, :, half + tile :]


SMEM = pl.BlockSpec(memory_space=pltpu.SMEM)
VMEM = pl.BlockSpec(memory_space=pltpu.VMEM)
HBM = pl.BlockSpec(memory_space=pltpu.HBM)


def work_buffers(slots, size):
    return [
        pltpu.VMEM((2 * size, slots * size), jnp.bfloat16),
        pltpu.VMEM((2 * size, slots * size), jnp.bfloat16),
        pltpu.VMEM((size, 2 * size), jnp.float32),
        pltpu.VMEM((slots, 2 * size, size), jnp.float32),
    ]


def kernel_options(slots, size):
    return dict(
        compiler_params=pltpu.CompilerParams(vmem_limit_bytes=8 * 1024 * 1024),
        cost_estimate=pl.CostEstimate(
            flops=slots * 48 * size**3, bytes_accessed=6 * 1024 * 1024, transcendentals=0
        ),
    )


def forward(offsets, info, padded, probe_re, probe_im, tables, measured, gain, dark, good, blocks):
    slots, size = measured.shape[:2]
    depth = 4 * (size // blocks) + SUBLANES
    return pl.pallas_call(
        forward_kernel,
        out_shape=(
            jax.ShapeDtypeStruct((blocks // 2, depth, size), jnp.float32),
            jax.ShapeDtypeStruct((blocks // 2, depth, size), jnp.float32),
            jax.ShapeDtypeStruct((slots * size, 2 * size), jnp.bfloat16),
            jax.ShapeDtypeStruct((slots * size, 2 * size), jnp.bfloat16),
            jax.ShapeDtypeStruct((slots, 2, size, size), jnp.float32),
        ),
        in_specs=[SMEM] * 2 + [VMEM] * 7 + [HBM] * 4,
        out_specs=(VMEM,) * 5,
        scratch_shapes=[
            pltpu.VMEM((blocks, depth, size), jnp.float32),
            pltpu.VMEM((slots, size, size), jnp.float32),
            pltpu.VMEM((size, size), jnp.float32),
            pltpu.VMEM((size, size), jnp.float32),
            pltpu.VMEM((size, size), jnp.int32),
            pltpu.SemaphoreType.DMA((4,)),
            *work_buffers(slots, size),
        ],
        name="forward",
        **kernel_options(slots, size),
    )(offsets, info, padded, probe_re, probe_im, *tables, measured, gain, dark, good)


def backward(offsets, info, x_high, x_low, win, probe_re, probe_im, tables, tile, blocks):
    slots, _, size, _ = win.shape
    half = size // 2
    side = tile + size
    depth = 2 * (size // blocks)
    return pl.pallas_call(
        backward_kernel,
        out_shape=(
            jax.ShapeDtypeStruct((blocks // 2, depth, size), jnp.float32),
            jax.ShapeDtypeStruct((blocks // 2, depth, size), jnp.float32),
            jax.ShapeDtypeStruct((3, side, half), jnp.float32),
            jax.ShapeDtypeStruct((3, side, tile), jnp.float32),
            jax.ShapeDtypeStruct((3, side, half), jnp.float32),
        ),
        in_specs=[SMEM] * 2 + [VMEM] * 9,
        out_specs=(VMEM,) * 5,
        scratch_shapes=[
            pltpu.VMEM((blocks, depth, size), jnp.float32),
            pltpu.VMEM((3, side, side), jnp.float32),
            *work_buffers(slots, size),
        ],
        name="backward",
        **kernel_options(slots, size),
    )(offsets, info, x_high, x_low, win, probe_re, probe_im, *tables)


def exchange_steps(n_tx, n_ty, n_pa):
    def along(dim, bit):
        def partner(*here):
            return tuple(at ^ bit if k == dim else at for k, at in enumerate(here))

        def upper(*here):
            return (here[dim] // bit) & 1

        return partner, upper

    def by_core(one, two):
        def partner(t, y, p):
            return one[0](t, y, p) if y % 2 == 0 else two[0](t, y, p)

        def upper(t, y, p):
            return jnp.where(y % 2 == 0, one[1](t, y, p), two[1](t, y, p))

        return partner, upper

    tx, ty, pa = (
        [along(dim, 1 << k) for k in range(low, size.bit_length() - 1)]
        for dim, (low, size) in enumerate(((0, n_tx), (1, n_ty), (0, n_pa)))
    )
    halving = [along(1, 1)]
    whole = []
    while tx and pa and len(halving) < 3:
        one, two = pa.pop(0), tx.pop(0)
        halving += [by_core(one, two), by_core(two, one)]
    while tx and ty:
        one, two = ty.pop(0), tx.pop(0)
        whole += [by_core(one, two), by_core(two, one)]
    whole += tx + ty + pa
    return halving, whole


def update(
    object_re,
    object_im,
    probe_real,
    probe_imaginary,
    gain,
    dark,
    measured,
    positions,
    counts,
    pixel_good,
):
    tile_side = object_re.shape[0]
    window = probe_real.shape[0]
    half = window // 2
    tables = dft_tables(window)
    t, y, p = (lax.axis_index(axis) for axis in MESH_AXES)
    n_tx, n_ty, n_pa = (lax.axis_size(axis) for axis in MESH_AXES)

    tile = lax.optimization_barrier(jnp.stack([object_re, object_im]))
    near = neighbour_swap(tile, "tx", 0)
    far = neighbour_swap(tile, "tx", 1)
    before, after = ordered(t % 2, far, near)
    strip = jnp.concatenate([before, tile, after], axis=1)
    near = neighbour_swap(strip, "ty", 0)
    far = neighbour_swap(strip, "ty", 1)
    before, after = ordered(y % 2, far, near)
    padded = jnp.concatenate([before, strip, after], axis=2)
    anchor = jnp.stack([t * tile_side, y * tile_side]).astype(jnp.int32)
    offsets = positions - anchor

    halving, whole = exchange_steps(n_tx, n_ty, n_pa)
    blocks = 1 << len(halving)
    span = window // blocks

    def block_of(t, y, p):
        place = jnp.int32(0)
        for _, bit in halving:
            place = 2 * place + bit(t, y, p)
        return place

    mine = block_of(t, y, p)
    other = block_of(*halving[0][0](t, y, p))
    info = jnp.stack([counts[0], mine, other, y % 2]).astype(jnp.int32)
    *early, x_high, x_low, win = forward(
        offsets, info, padded, probe_real, probe_imaginary, tables,
        measured, gain, dark, pixel_good, blocks,
    )
    *late, to_one, inner, to_zero = backward(
        offsets, info, x_high, x_low, win, probe_real, probe_imaginary, tables,
        tile_side, blocks,
    )

    def first_half(kept, sent):
        return kept + partner_swap(sent, halving[0][0])

    early = first_half(*early)
    late = first_half(*late)
    sums = jnp.concatenate([late, early], axis=1)
    for k, (partner, _) in enumerate(halving[1:], 1):
        middle = sums.shape[0] // 2
        sums = sums[:middle] + partner_swap(sums[middle:], partner)
    for partner, _ in whole:
        sums = sums + partner_swap(sums, partner)
    sums = sums[0]

    def own(array):
        return lax.dynamic_slice_in_dim(array, mine * span, span, 0)

    probe_num = sums[: 2 * span].reshape(2, span, window)
    power, gain_num, gain_den, dark_num = sums[2 * span : 6 * span].reshape(4, span, window)
    dark_den = own(pixel_good).astype(jnp.float32) * sums[6 * span : 6 * span + 1]
    new = jnp.stack(
        [
            own(probe_real) + probe_num[0] / (power + 0.5),
            own(probe_imaginary) + probe_num[1] / (power + 0.5),
            own(gain) + gain_num / (gain_den + 1.0),
            own(dark) + 0.5 * dark_num / (dark_den + 1.0),
        ]
    )
    for k, (partner, bit) in reversed(list(enumerate(halving))):
        low, high = ordered(bit(t, y, p), new, partner_swap(new, partner))
        new = jnp.concatenate([low, high], axis=1)

    edge = half + tile_side
    from_zero = neighbour_swap(to_zero, "ty", 0)
    from_one = neighbour_swap(to_one, "ty", 1, fill=False)
    strip = inner + from_zero + from_one
    to_one, to_zero = ordered(t % 2, strip[:, :half], strip[:, edge:])
    from_zero = neighbour_swap(to_zero, "tx", 0)
    from_one = neighbour_swap(to_one, "tx", 1)
    sums = strip[:, half:edge] + from_zero + from_one
    for k in range(n_pa.bit_length() - 2, -1, -1):
        bit = 1 << k
        rows = sums.shape[1] // 2
        upper = (p // bit) & 1
        kept = lax.dynamic_slice_in_dim(sums, upper * rows, rows, 1)
        sent = lax.dynamic_slice_in_dim(sums, (1 - upper) * rows, rows, 1)
        sums = kept + lax.ppermute(sent, "pa", [(i, i ^ bit) for i in range(n_pa)])
    rows = sums.shape[1]
    own_tile = lax.dynamic_slice_in_dim(tile, p * rows, rows, 1)
    new_re = own_tile[0] + sums[0] / (sums[2] + 0.5)
    new_im = own_tile[1] + sums[1] / (sums[2] + 0.5)
    return (new_re, new_im, new[0], new[1], new[2], new[3])


def solution(mesh):
    placed = (
        P("tx", "ty"),
        P("tx", "ty"),
        P(),
        P(),
        P(),
        P(),
        P(("tx", "ty", "pa"), None, None),
        P(("tx", "ty", "pa"), None),
        P(("tx", "ty", "pa")),
        P(),
    )
    return jax.shard_map(
        update,
        mesh=mesh,
        in_specs=placed,
        out_specs=(P(("tx", "pa"), "ty"), P(("tx", "pa"), "ty"), P(), P(), P(), P()),
        check_vma=False,
    )
```

```python
import functools
import math

import jax
import jax.numpy as jnp
import numpy as np
from jax import lax
from jax.experimental import pallas as pl
from jax.experimental.pallas import tpu as pltpu
from jax.sharding import PartitionSpec as P


MESH_AXES = ("tx", "ty", "pa")
ROWS = 32
SUBLANES = 8
SMEM = pl.BlockSpec(memory_space=pltpu.SMEM)
VMEM = pl.BlockSpec(memory_space=pltpu.VMEM)
HBM = pl.BlockSpec(memory_space=pltpu.HBM)


def partner_swap(value, partner_of):
    shape = tuple(lax.axis_size(axis) for axis in MESH_AXES)
    moves = []
    for here in np.ndindex(*shape):
        there = partner_of(*here)
        if there != here:
            source, target = (int(np.ravel_multi_index(at, shape)) for at in (here, there))
            moves.append((source, target))
    return lax.ppermute(value, MESH_AXES, moves)


def neighbour_swap(value, axis, parity, fill=True):
    dim = MESH_AXES.index(axis)
    size = lax.axis_size(axis)
    n_pa = lax.axis_size("pa")

    def paired(at):
        other = (at - parity ^ 1) + parity
        return other if 0 <= other < size else None

    def partner(*here):
        other = paired(here[dim])
        if other is None:
            idle = here[2] ^ 1
            return (here[0], here[1], idle if fill and idle < n_pa else here[2])
        return tuple(other if k == dim else at for k, at in enumerate(here))

    got = partner_swap(value, partner)
    if not fill or all(paired(at) is not None for at in range(size)):
        return got
    other = (lax.axis_index(axis) - parity ^ 1) + parity
    return jnp.where((0 <= other) & (other < size), got, 0.0)


def ordered(parity, first, second):
    even = parity == 0
    return jnp.where(even, first, second), jnp.where(even, second, first)


def split_table(table):
    high = table.astype(jnp.bfloat16)
    low = (table - high.astype(np.float32)).astype(jnp.bfloat16)
    return high, low


def dft_tables(size):
    index = np.arange(size)
    angle = (np.outer(index, index) % size) * (2.0 * math.pi / size)
    real = (np.cos(angle) / math.sqrt(size)).astype(np.float32)
    imag = (-np.sin(angle) / math.sqrt(size)).astype(np.float32)
    row_form = np.block([[real, imag], [-imag, real]])
    col_form = np.block([[real, -imag], [imag, real]])
    return np.stack([*split_table(row_form), *split_table(col_form)])


def split(value):
    high = value.astype(jnp.bfloat16)
    return high, (value - high.astype(jnp.float32)).astype(jnp.bfloat16)


def three_pass(left_high, left_low, right_high, right_low):
    dot = functools.partial(jnp.dot, preferred_element_type=jnp.float32)
    return dot(left_high, right_high) + dot(left_high, right_low) + dot(left_low, right_high)


def aligned(row):
    part = lax.rem(row, SUBLANES)
    return row - part, part


def right_then_left(which, first_high, first_low, second_high, second_low, x_high, x_low, y_high, y_low, line, plane):
    size = plane.shape[2]
    for slot in which:
        here = pl.ds(slot * size, size)
        line[slot] = three_pass(x_high[here, :], x_low[here, :], first_high[...], first_low[...])
        for part in range(2):
            high, low = split(line[slot, :, part * size : (part + 1) * size])
            y_high[part * size : (part + 1) * size, here] = high
            y_low[part * size : (part + 1) * size, here] = low
        plane[slot] = three_pass(second_high[...], second_low[...], y_high[:, here], y_low[:, here])


def put_x(x_high, x_low, slot, size, at, real, imag):
    rows = pl.ds(slot * size + at, ROWS)
    for part, value in enumerate((real, imag)):
        high, low = split(value)
        x_high[rows, part * size : (part + 1) * size] = high
        x_low[rows, part * size : (part + 1) * size] = low


def put_sums(sums, info, step, values):
    blocks, _, size = sums.shape
    span = size // blocks
    half = blocks // 2
    for sub in range(ROWS // span):
        block = step * (ROWS // span) + sub
        mine = lax.bitwise_xor(block, info[1])
        place = jnp.where(mine < half, mine, half + lax.bitwise_xor(block, info[2]))
        for kind, value in enumerate(values):
            sums[place, kind * span : (kind + 1) * span, :] = value[sub * span : (sub + 1) * span]


def forward_kernel(
    offsets,
    info,
    padded,
    probe_re,
    probe_im,
    tables,
    measured,
    gain,
    dark,
    good,
    kept,
    sent,
    x_high,
    x_low,
    win,
    sums,
    y_high,
    y_low,
    line,
    plane,
):
    slots = measured.shape[0]
    size = probe_re.shape[0]
    side = padded.shape[1]
    steps = size // ROWS
    for slot in range(slots):
        row, row_part = aligned(offsets[slot, 0])
        back_rows = lax.rem(ROWS + SUBLANES - row_part, ROWS + SUBLANES)
        back_cols = lax.rem(side - offsets[slot, 1], side)

        def load(step):
            at = step * ROWS
            here = pl.ds(at, ROWS)
            parts = []
            for part in range(2):
                band = padded[part, pl.ds(pl.multiple_of(row + at, SUBLANES), ROWS + SUBLANES), :]
                band = pltpu.roll(band, back_rows, axis=0)[:ROWS]
                parts.append(pltpu.roll(band, back_cols, axis=1)[:, :size])
                win[slot, part, here, :] = parts[part]
            wr, wi = parts
            pr, pi = probe_re[here, :], probe_im[here, :]
            put_x(x_high, x_low, slot, size, at, pr * wr - pi * wi, pr * wi + pi * wr)

        for step in range(steps):
            load(step)
        right_then_left(
            (slot,), *(tables.at[k] for k in (0, 1, 2, 3)), x_high, x_low, y_high, y_low, line, plane
        )

    blocks, depth, _ = sums.shape
    live_rows = jnp.full((SUBLANES, size), info[0].astype(jnp.float32), jnp.float32)
    for block in range(blocks):
        sums[block, depth - SUBLANES :, :] = live_rows

    def detect(step):
        at = step * ROWS
        here = pl.ds(at, ROWS)
        valid = good[here, :].astype(jnp.float32)
        values = [0.0] * 4
        for slot in range(slots):
            live = jnp.where(slot < info[0], 1.0, 0.0).astype(jnp.float32)
            fr = plane[slot, here, :]
            fi = plane[slot, pl.ds(size + at, ROWS), :]
            inten = fr * fr + fi * fi
            model = gain[here, :] * inten + dark[here, :]
            seen = measured[slot, here, :]
            ratio = valid * (jnp.sqrt(seen / model) - 1.0)
            put_x(x_high, x_low, slot, size, at, ratio * fr, ratio * fi)
            weight = valid * live
            resid = weight * (seen - model)
            wr, wi = win[slot, 0, here, :], win[slot, 1, here, :]
            terms = (live * (wr * wr + wi * wi), resid * inten, weight * inten * inten, resid)
            values = [value + term for value, term in zip(values, terms)]
        put_sums(sums, info, step, values)

    for step in range(steps):
        detect(step)
    kept[...] = sums[: blocks // 2]
    sent[...] = sums[blocks // 2 :]


def stage_kernel(*refs):
    count = (len(refs) - 1) // 2
    copies = [
        pltpu.make_async_copy(source, target, refs[-1].at[k])
        for k, (source, target) in enumerate(zip(refs[:count], refs[count : 2 * count]))
    ]
    for copy in copies:
        copy.start()
    for copy in copies:
        copy.wait()


def stage(*arrays):
    return pl.pallas_call(
        stage_kernel,
        out_shape=tuple(jax.ShapeDtypeStruct(a.shape, a.dtype) for a in arrays),
        in_specs=[HBM] * len(arrays),
        out_specs=(VMEM,) * len(arrays),
        scratch_shapes=[pltpu.SemaphoreType.DMA((len(arrays),))],
        compiler_params=pltpu.CompilerParams(vmem_limit_bytes=1024 * 1024),
        name="stage",
    )(*arrays)


def backward_kernel(
    info,
    x_high,
    x_low,
    win,
    tables,
    kept,
    sent,
    plane,
    sums,
    y_high,
    y_low,
    line,
):
    slots, _, size, _ = win.shape
    right_then_left(
        range(slots), *(tables.at[k] for k in (2, 3, 0, 1)), x_high, x_low, y_high, y_low, line, plane
    )
    for step in range(size // ROWS):
        at = step * ROWS
        here = pl.ds(at, ROWS)
        values = [0.0] * 2
        for slot in range(slots):
            live = jnp.where(slot < info[0], 1.0, 0.0).astype(jnp.float32)
            br = live * plane[slot, here, :]
            bi = live * plane[slot, pl.ds(size + at, ROWS), :]
            wr, wi = win[slot, 0, here, :], win[slot, 1, here, :]
            values = [values[0] + wr * br + wi * bi, values[1] + wr * bi - wi * br]
        put_sums(sums, info, step, values)
    kept[...] = sums[: sums.shape[0] // 2]
    sent[...] = sums[sums.shape[0] // 2 :]


def place_kernel(
    offsets,
    info,
    plane,
    probe_re,
    probe_im,
    to_one,
    inner,
    to_zero,
    accum,
):
    slots, _, size = plane.shape
    side = accum.shape[1]
    tile = inner.shape[2]
    half = to_one.shape[2]
    accum[...] = jnp.zeros_like(accum)
    for step in range(size // ROWS):
        at = step * ROWS
        here = pl.ds(at, ROWS)
        pr, pi = probe_re[here, :], probe_im[here, :]
        power = pr * pr + pi * pi
        for slot in range(slots):
            live = jnp.where(slot < info[0], 1.0, 0.0).astype(jnp.float32)
            row, row_part = aligned(offsets[slot, 0])
            col = offsets[slot, 1]
            br = live * plane[slot, here, :]
            bi = live * plane[slot, pl.ds(size + at, ROWS), :]
            there = pl.ds(pl.multiple_of(row + at, SUBLANES), ROWS + SUBLANES)
            for part, term in enumerate((pr * br + pi * bi, pr * bi - pi * br, live * power)):
                wide = jnp.pad(term, ((0, SUBLANES), (0, side - size)))
                wide = pltpu.roll(pltpu.roll(wide, row_part, axis=0), col, axis=1)
                accum[part, there, :] += wide
    odd = info[3] == 1
    inner[...] = accum[:, :, half : half + tile]

    @pl.when(odd)
    def _():
        to_one[...] = accum[:, :, half + tile :]
        to_zero[...] = accum[:, :, :half]

    @pl.when(jnp.logical_not(odd))
    def _():
        to_one[...] = accum[:, :, :half]
        to_zero[...] = accum[:, :, half + tile :]


def work_buffers(slots, size):
    return [
        pltpu.VMEM((2 * size, slots * size), jnp.bfloat16),
        pltpu.VMEM((2 * size, slots * size), jnp.bfloat16),
        pltpu.VMEM((slots, size, 2 * size), jnp.float32),
        pltpu.VMEM((slots, 2 * size, size), jnp.float32),
    ]


def kernel_options(slots, size):
    return dict(
        compiler_params=pltpu.CompilerParams(vmem_limit_bytes=8 * 1024 * 1024),
        cost_estimate=pl.CostEstimate(
            flops=slots * 48 * size**3, bytes_accessed=6 * 1024 * 1024, transcendentals=0
        ),
    )


def forward(offsets, info, padded, probe_re, probe_im, tables, measured, gain, dark, good, blocks):
    slots, size = measured.shape[:2]
    depth = 4 * (size // blocks) + SUBLANES
    return pl.pallas_call(
        forward_kernel,
        out_shape=(
            jax.ShapeDtypeStruct((blocks // 2, depth, size), jnp.float32),
            jax.ShapeDtypeStruct((blocks // 2, depth, size), jnp.float32),
            jax.ShapeDtypeStruct((slots * size, 2 * size), jnp.bfloat16),
            jax.ShapeDtypeStruct((slots * size, 2 * size), jnp.bfloat16),
            jax.ShapeDtypeStruct((slots, 2, size, size), jnp.float32),
        ),
        in_specs=[SMEM] * 2 + [VMEM] * 8,
        out_specs=(VMEM,) * 5,
        scratch_shapes=[
            pltpu.VMEM((blocks, depth, size), jnp.float32),
            *work_buffers(slots, size),
        ],
        name="forward",
        **kernel_options(slots, size),
    )(offsets, info, padded, probe_re, probe_im, tables, measured, gain, dark, good)


def backward(info, x_high, x_low, win, tables, blocks):
    slots, _, size, _ = win.shape
    depth = 2 * (size // blocks)
    return pl.pallas_call(
        backward_kernel,
        out_shape=(
            jax.ShapeDtypeStruct((blocks // 2, depth, size), jnp.float32),
            jax.ShapeDtypeStruct((blocks // 2, depth, size), jnp.float32),
            jax.ShapeDtypeStruct((slots, 2 * size, size), jnp.float32),
        ),
        in_specs=[SMEM] + [VMEM] * 4,
        out_specs=(VMEM,) * 3,
        scratch_shapes=[
            pltpu.VMEM((blocks, depth, size), jnp.float32),
            *work_buffers(slots, size)[:-1],
        ],
        name="backward",
        **kernel_options(slots, size),
    )(info, x_high, x_low, win, tables)


def place(offsets, info, plane, probe_re, probe_im, tile):
    size = probe_re.shape[0]
    half = size // 2
    side = tile + size
    return pl.pallas_call(
        place_kernel,
        out_shape=(
            jax.ShapeDtypeStruct((3, side, half), jnp.float32),
            jax.ShapeDtypeStruct((3, side, tile), jnp.float32),
            jax.ShapeDtypeStruct((3, side, half), jnp.float32),
        ),
        in_specs=[SMEM] * 2 + [VMEM] * 3,
        out_specs=(VMEM,) * 3,
        scratch_shapes=[pltpu.VMEM((3, side, side), jnp.float32)],
        name="place",
        **kernel_options(plane.shape[0], size),
    )(offsets, info, plane, probe_re, probe_im)


def exchange_steps(n_tx, n_ty, n_pa):
    def along(dim, bit):
        def partner(*here):
            return tuple(at ^ bit if k == dim else at for k, at in enumerate(here))

        def upper(*here):
            return (here[dim] // bit) & 1

        return partner, upper

    def by_core(one, two):
        def partner(t, y, p):
            return one[0](t, y, p) if y % 2 == 0 else two[0](t, y, p)

        def upper(t, y, p):
            return jnp.where(y % 2 == 0, one[1](t, y, p), two[1](t, y, p))

        return partner, upper

    tx, ty, pa = (
        [along(dim, 1 << k) for k in range(low, size.bit_length() - 1)]
        for dim, (low, size) in enumerate(((0, n_tx), (1, n_ty), (0, n_pa)))
    )
    halving = [along(1, 1)]
    whole = []
    while tx and pa and len(halving) < 3:
        one, two = pa.pop(0), tx.pop(0)
        halving += [by_core(one, two), by_core(two, one)]
    while tx and ty:
        one, two = ty.pop(0), tx.pop(0)
        whole += [by_core(one, two), by_core(two, one)]
    whole += tx + ty + pa
    return halving, whole


def update(
    object_re,
    object_im,
    probe_real,
    probe_imaginary,
    gain,
    dark,
    measured,
    positions,
    counts,
    pixel_good,
):
    tile_side = object_re.shape[0]
    window = probe_real.shape[0]
    half = window // 2
    tables = dft_tables(window)
    t, y, p = (lax.axis_index(axis) for axis in MESH_AXES)
    n_tx, n_ty, n_pa = (lax.axis_size(axis) for axis in MESH_AXES)

    tile = lax.optimization_barrier(jnp.stack([object_re, object_im]))
    near = neighbour_swap(tile, "tx", 0)
    far = neighbour_swap(tile, "tx", 1)
    before, after = ordered(t % 2, far, near)
    strip = jnp.concatenate([before, tile, after], axis=1)
    near = neighbour_swap(strip, "ty", 0)
    far = neighbour_swap(strip, "ty", 1)
    before, after = ordered(y % 2, far, near)
    padded = jnp.concatenate([before, strip, after], axis=2)
    anchor = jnp.stack([t * tile_side, y * tile_side]).astype(jnp.int32)
    offsets = positions - anchor

    halving, whole = exchange_steps(n_tx, n_ty, n_pa)
    blocks = 1 << len(halving)
    span = window // blocks

    def block_of(t, y, p):
        place = jnp.int32(0)
        for _, bit in halving:
            place = 2 * place + bit(t, y, p)
        return place

    mine = block_of(t, y, p)
    other = block_of(*halving[0][0](t, y, p))
    info = jnp.stack([counts[0], mine, other, y % 2]).astype(jnp.int32)
    tables, measured, probe_real, probe_imaginary, gain, dark, pixel_good = stage(
        jnp.asarray(tables), measured, probe_real, probe_imaginary, gain, dark, pixel_good
    )
    *early, x_high, x_low, win = forward(
        offsets, info, padded, probe_real, probe_imaginary, tables,
        measured, gain, dark, pixel_good, blocks,
    )
    *late, plane = backward(info, x_high, x_low, win, tables, blocks)
    to_one, inner, to_zero = place(
        offsets, info, plane, probe_real, probe_imaginary, tile_side
    )

    def first_half(kept, sent):
        return kept + partner_swap(sent, halving[0][0])

    early = first_half(*early)
    late = first_half(*late)
    sums = jnp.concatenate([late, early], axis=1)
    for k, (partner, _) in enumerate(halving[1:], 1):
        middle = sums.shape[0] // 2
        sums = sums[:middle] + partner_swap(sums[middle:], partner)
    for partner, _ in whole:
        sums = sums + partner_swap(sums, partner)
    sums = sums[0]

    def own(array):
        return lax.dynamic_slice_in_dim(array, mine * span, span, 0)

    probe_num = sums[: 2 * span].reshape(2, span, window)
    power, gain_num, gain_den, dark_num = sums[2 * span : 6 * span].reshape(4, span, window)
    dark_den = own(pixel_good).astype(jnp.float32) * sums[6 * span : 6 * span + 1]
    new = jnp.stack(
        [
            own(probe_real) + probe_num[0] / (power + 0.5),
            own(probe_imaginary) + probe_num[1] / (power + 0.5),
            own(gain) + gain_num / (gain_den + 1.0),
            own(dark) + 0.5 * dark_num / (dark_den + 1.0),
        ]
    )
    for k, (partner, bit) in reversed(list(enumerate(halving))):
        low, high = ordered(bit(t, y, p), new, partner_swap(new, partner))
        new = jnp.concatenate([low, high], axis=1)

    edge = half + tile_side
    from_zero = neighbour_swap(to_zero, "ty", 0)
    from_one = neighbour_swap(to_one, "ty", 1, fill=False)
    strip = inner + from_zero + from_one
    to_one, to_zero = ordered(t % 2, strip[:, :half], strip[:, edge:])
    from_zero = neighbour_swap(to_zero, "tx", 0)
    from_one = neighbour_swap(to_one, "tx", 1)
    sums = strip[:, half:edge] + from_zero + from_one
    for k in range(n_pa.bit_length() - 2, -1, -1):
        bit = 1 << k
        rows = sums.shape[1] // 2
        upper = (p // bit) & 1
        kept = lax.dynamic_slice_in_dim(sums, upper * rows, rows, 1)
        sent = lax.dynamic_slice_in_dim(sums, (1 - upper) * rows, rows, 1)
        sums = kept + lax.ppermute(sent, "pa", [(i, i ^ bit) for i in range(n_pa)])
    rows = sums.shape[1]
    own_tile = lax.dynamic_slice_in_dim(tile, p * rows, rows, 1)
    new_re = own_tile[0] + sums[0] / (sums[2] + 0.5)
    new_im = own_tile[1] + sums[1] / (sums[2] + 0.5)
    return (new_re, new_im, new[0], new[1], new[2], new[3])


def solution(mesh):
    placed = (
        P("tx", "ty"),
        P("tx", "ty"),
        P(),
        P(),
        P(),
        P(),
        P(("tx", "ty", "pa"), None, None),
        P(("tx", "ty", "pa"), None),
        P(("tx", "ty", "pa")),
        P(),
    )
    return jax.shard_map(
        update,
        mesh=mesh,
        in_specs=placed,
        out_specs=(P(("tx", "pa"), "ty"), P(("tx", "pa"), "ty"), P(), P(), P(), P()),
        check_vma=False,
    )
```
